512 devices in a mesh: gx: 8 (over z), gy: 8 (over y), gz: 8 (over x, core).
Axes of the slice: x: 4, y: 8, z: 8, core: 2. Of those that a mesh axis runs over, the one named last changes fastest.
Arguments:
- basis: bfloat16 [32, 128, 64, 1024], P(None, 'gx', 'gy', 'gz'), may hold values from -12 to 12
- krylov: float32 [16, 128, 64, 1024], P(None, 'gx', 'gy', 'gz'), may hold values from -12 to 12
- center: bfloat16 [128, 64, 1024], P('gx', 'gy', 'gz'), may hold values from 8 to 24
- couplings: bfloat16 [26, 128, 64, 1024], P(None, 'gx', 'gy', 'gz'), may hold values from -1 to 0.3984375
Outputs:
- projected: float32 [16, 128, 64, 1024], P(None, 'gx', 'gy', 'gz')
- coefficients: float32 [32, 16], replicated
The draws below stay inside these ranges and needn't reach their ends.
All inputs are finite; a program needn't handle non-finite values.
Results may differ from the reference program's by a relative error of at most 0.0003.
Values sent between devices are 32-bit elements; how exact they have to be, the bound alone decides.
No kernel may reach another device: no remote copies, remote signals or barrier semaphores. Data moves between devices by JAX's collectives and lax.ppermute only.
A program may use at most 64 MiB of HBM per device.

```python
import math
import jax
import jax.numpy as jnp
from jax import lax

NU = 32
NV = 16
NX = 128
NY = 64
NZ = 1024


def basis_field(key):
    base = jax.random.fold_in(key, 11)
    key_raw, key_mix = jax.random.split(base)
    raw = jnp.clip(jax.random.normal(key_raw, (NU, NX, NY, NZ), jnp.float32), -4.0, 4.0)
    envelope = 1.0 + 2.0 * jnp.arange(NX, dtype=jnp.float32) / (NX - 1)
    field = (raw * envelope[None, :, None, None]).reshape(NU, -1)
    scale = 1.0 / (NX * NY * NZ)
    gram = scale * jnp.dot(field, field.T, precision=lax.Precision.HIGHEST)
    lower = jnp.linalg.cholesky(gram)
    ortho = lax.linalg.triangular_solve(lower, field, left_side=True, lower=True)
    bend = jnp.eye(NU, dtype=jnp.float32) + 0.04 * jax.random.normal(key_mix, (NU, NU), jnp.float32)
    mixed = jnp.dot(bend, ortho, precision=lax.Precision.HIGHEST)
    return mixed.reshape(NU, NX, NY, NZ)


def draw_basis(key, part):
    return jnp.clip(basis_field(key), -12.0, 12.0).astype(jnp.bfloat16)


def draw_krylov(key, part):
    field = jnp.clip(basis_field(key), -12.0, 12.0).astype(jnp.bfloat16).astype(jnp.float32)
    key_mix, key_noise = jax.random.split(jax.random.fold_in(key, 23))
    mixing = 0.3 * jax.random.normal(key_mix, (NU, NV), jnp.float32)
    noise = jax.random.normal(key_noise, (NV, NX, NY, NZ), jnp.float32)
    return jnp.clip(jnp.einsum('ij,ixyz->jxyz', mixing, field) + noise, -12.0, 12.0)


def block_scale(rng, shape, cuts, least, high):
    level = 1.0
    for position, blocks in cuts:
        steps = jax.random.uniform(jax.random.fold_in(jax.random.fold_in(rng, 6), position), (blocks,), jnp.float32, least / len(cuts), high / len(cuts))
        level = level * jnp.repeat(jnp.exp(steps), shape[position] // blocks).reshape((-1,) + (1,) * (len(shape) - 1 - position))
    return level


def setup_inputs(seed: int = 0) -> dict:
    key_of = jax.random.split(jax.random.key(seed), 5)
    return {
        "basis": draw_basis(jax.random.fold_in(key_of[4], 71), 0),
        "krylov": draw_krylov(jax.random.fold_in(key_of[4], 71), 0),
        "center": jnp.clip(jnp.exp(math.log(24.0) - 1.0986123 * jax.random.uniform(key_of[2], (NX, NY, NZ), jnp.float32) ** block_scale(key_of[2], (NX, NY, NZ), ((0, 8), (1, 8), (2, 8)), -0.2, 0.2)), 8.0, 24.0).astype(jnp.bfloat16),
        "couplings": jnp.clip(-1.0 + 1.3984375 * jax.random.uniform(key_of[3], (26, NX, NY, NZ), jnp.float32) ** block_scale(key_of[3], (26, NX, NY, NZ), ((1, 8), (2, 8), (3, 8)), -0.2, 0.2), -1.0, 0.3984375).astype(jnp.bfloat16),
    }


def apply_single(vector, center, couplings):
    padded = jnp.pad(vector, 1)
    result = center.astype(jnp.float32) * vector
    which = 0
    for step_a in (-1, 0, 1):
        for step_b in (-1, 0, 1):
            for step_c in (-1, 0, 1):
                if step_a == 0 and step_b == 0 and (step_c == 0):
                    continue
                moved = padded[1 + step_a:1 + step_a + NX, 1 + step_b:1 + step_b + NY, 1 + step_c:1 + step_c + NZ]
                result = result + couplings[which].astype(jnp.float32) * moved
                which = which + 1
    return result

def reference(basis, krylov, center, couplings):
    image = lax.map(lambda vector: apply_single(vector, center, couplings), krylov)
    scale = 1.0 / (NX * NY * NZ)
    flat_basis = basis.reshape(NU, -1).astype(jnp.float32)
    flat_image = image.reshape(NV, -1)
    dims = (((1,), (1,)), ((), ()))
    first = scale * lax.dot_general(flat_basis.astype(jnp.float32), flat_image.astype(jnp.float32), dims, precision=lax.Precision.HIGHEST, preferred_element_type=jnp.float32)
    once = flat_image - jnp.dot(first.T.astype(jnp.float32), flat_basis.astype(jnp.float32), precision=lax.Precision.HIGHEST, preferred_element_type=jnp.float32)
    second = scale * lax.dot_general(flat_basis.astype(jnp.float32), once.astype(jnp.float32), dims, precision=lax.Precision.HIGHEST, preferred_element_type=jnp.float32)
    projected = once - jnp.dot(second.T.astype(jnp.float32), flat_basis.astype(jnp.float32), precision=lax.Precision.HIGHEST, preferred_element_type=jnp.float32)
    return (projected.reshape(NV, NX, NY, NZ), first + second)
```

```python
import jax
import jax.numpy as jnp
from jax import lax
from jax.sharding import PartitionSpec as P


def extended(block, sides, width):
    for axis, dim in sides:
        count = lax.axis_size(axis)
        forward = [(i, i + 1) for i in range(count - 1)]
        backward = [(target, source) for source, target in forward]
        low = lax.ppermute(
            lax.slice_in_dim(block, block.shape[dim] - width, None, axis=dim), axis, forward
        )
        high = lax.ppermute(lax.slice_in_dim(block, 0, width, axis=dim), axis, backward)
        block = jnp.concatenate([low, block, high], axis=dim)
    return block


def summed(values, axes):
    count = 1
    for axis in axes:
        count *= lax.axis_size(axis)
    copies = jnp.broadcast_to(values[None], (count,) + values.shape)
    return lax.all_to_all(copies, axes, 0, 0).sum(0)


def local(basis, krylov, center, couplings):
    count_v, size_x, size_y, size_z = krylov.shape
    count_u = basis.shape[0]
    padded = extended(krylov, (("gx", 1), ("gy", 2), ("gz", 3)), 1)
    image = center.astype(jnp.float32)[None] * krylov
    which = 0
    for step_a in (-1, 0, 1):
        for step_b in (-1, 0, 1):
            for step_c in (-1, 0, 1):
                if step_a == 0 and step_b == 0 and (step_c == 0):
                    continue
                moved = padded[
                    :,
                    1 + step_a : 1 + step_a + size_x,
                    1 + step_b : 1 + step_b + size_y,
                    1 + step_c : 1 + step_c + size_z,
                ]
                image = image + couplings[which].astype(jnp.float32)[None] * moved
                which = which + 1
    total_cells = (
        size_x * size_y * size_z * lax.axis_size("gx") * lax.axis_size("gy") * lax.axis_size("gz")
    )
    scale = 1.0 / total_cells
    flat_basis = basis.reshape(count_u, -1)
    flat_image = image.reshape(count_v, -1)
    dims = (((1,), (1,)), ((), ()))
    high = lax.Precision.HIGHEST
    gram = lax.dot_general(flat_basis, flat_basis, dims, preferred_element_type=jnp.float32)
    part = lax.dot_general(
        flat_basis, flat_image, dims, precision=high, preferred_element_type=jnp.float32
    )
    payload = (scale * jnp.concatenate([gram, part], axis=1)).reshape(-1, 128)
    payload = summed(payload, ("gz",))
    payload = summed(payload, ("gx", "gy"))
    payload = payload.reshape(count_u, count_u + count_v)
    gram, first = payload[:, :count_u], payload[:, count_u:]
    coefficients = first + (first - jnp.dot(gram, first, precision=high))
    projected = flat_image - jnp.dot(
        coefficients.T, flat_basis, precision=high, preferred_element_type=jnp.float32
    )
    return (projected.reshape(count_v, size_x, size_y, size_z), coefficients)


def solution(mesh):
    in_specs = (
        P(None, "gx", "gy", "gz"),
        P(None, "gx", "gy", "gz"),
        P("gx", "gy", "gz"),
        P(None, "gx", "gy", "gz"),
    )
    out_specs = (P(None, "gx", "gy", "gz"), P())
    return jax.shard_map(local, mesh=mesh, in_specs=in_specs, out_specs=out_specs, check_vma=False)
```

```python
import jax
import jax.numpy as jnp
import numpy as np
from jax import lax
from jax.experimental import pallas as pl
from jax.experimental.pallas import tpu as pltpu
from jax.sharding import PartitionSpec as P

F32 = jnp.float32
BF16 = jnp.bfloat16
NT = (((1,), (1,)), ((), ()))
STEPS = (-1, 0, 1)


def call(name, body, out, scratch=(), flops=0, data=0, aliases=None):
    single = not isinstance(out, (tuple, list))
    shapes = (out,) if single else tuple(out)
    built = pl.pallas_call(
        body,
        name=name,
        out_shape=shapes[0] if single else shapes,
        scratch_shapes=list(scratch),
        input_output_aliases=aliases or {},
        compiler_params=pltpu.CompilerParams(vmem_limit_bytes=40 << 20),
        cost_estimate=pl.CostEstimate(flops=flops, bytes_accessed=data, transcendentals=0),
    )
    return built


def like(shape, dtype=F32):
    return jax.ShapeDtypeStruct(shape, dtype)


def roll(value, shift, axis):
    size = value.shape[axis]
    shift = shift % size
    return value if shift == 0 else pltpu.roll(value, shift, axis)


def lanes(shape):
    return lax.broadcasted_iota(jnp.int32, shape, len(shape) - 1)


def rows(shape):
    return lax.broadcasted_iota(jnp.int32, shape, len(shape) - 2)


def spread(terms):
    total = None
    for c in STEPS:
        part = terms[0, c] + roll(terms[-1, c], 1, 0) + roll(terms[1, c], -1, 0)
        part = roll(part, -c, 1)
        total = part if total is None else total + part
    return total


def y_faces(krylov, low, high):
    low[...] = krylov[:, :, 0, :]
    high[...] = krylov[:, :, 7, :]


def number(a, b, c):
    k = (a + 1) * 9 + (b + 1) * 3 + (c + 1)
    return k if k < 13 else k - 1


def interior(krylov, center, couplings, image, z_high, z_low, face_x, face_y, face_z, weights, flat):
    lane = lanes((8, 128))
    row = rows((8, 128))
    slot = lanes((8, 128)) % 32

    def prepare(x, carry):
        edge_of = {}
        for a in STEPS:
            for b in STEPS:
                for c in STEPS:
                    index = (a + 1) * 9 + (b + 1) * 3 + (c + 1)
                    if (a, b, c) == (0, 0, 0):
                        value = center[x].astype(F32)
                    else:
                        value = couplings[number(a, b, c), x].astype(F32)
                    edge_of[a, b, c] = value
                    if c == -1:
                        value = jnp.where(lane == 0, 0.0, value)
                    if c == 1:
                        value = jnp.where(lane == 127, 0.0, value)
                    value = roll(value, c, 1)
                    if b != 0:
                        flat[(a + 1) * 6 + (b + 1) // 2 * 3 + (c + 1), x] = value
                        value = jnp.where(row == (0 if b == -1 else 7), 0.0, value)
                    value = roll(value, b, 0)
                    weights[index, x] = value
        for a in STEPS:
            for b in STEPS:
                both = jnp.where(lane == 127, edge_of[a, b, 1], edge_of[a, b, -1])
                for side, start in ((0, 0), (1, 127)):
                    moved = pltpu.roll(both, (x + 1 + 128 - start) % 128, 1)
                    k = (a + 1) * 3 + b + 1
                    face_z[side, k] = jnp.where(lane == x + 1, moved, face_z[side, k])
        return carry

    face_z[...] = jnp.zeros_like(face_z)
    lax.fori_loop(0, 16, prepare, 0)
    for side in range(2):
        for k in range(9):
            value = face_z[side, k]
            value = value + roll(value, 32, 1)
            face_z[side, k] = value + roll(value, 64, 1)
    zero = jnp.zeros((8, 128), F32)
    for k in range(9):
        face_x[0, k] = weights[k, 0]
        face_x[1, k] = weights[18 + k, 15]
        weights[k, 0] = zero
        weights[18 + k, 15] = zero
    for a in range(3):
        for c in range(3):
            face_y[0, a * 3 + c] = flat[a * 6 + c, :, 0, :]
            face_y[1, a * 3 + c] = flat[a * 6 + 3 + c, :, 7, :]

    z_high[...] = jnp.zeros_like(z_high)
    z_low[...] = jnp.zeros_like(z_low)

    def plane(x, carry):
        before = jnp.maximum(x - 1, 0)
        after = jnp.minimum(x + 1, 15)
        for group in range(4):
            high = z_high[group]
            low = z_low[group]
            for inner in range(4):
                j = group * 4 + inner
                source = {-1: krylov[j, before], 0: krylov[j, x], 1: krylov[j, after]}
                terms = {}
                for b in STEPS:
                    for c in STEPS:
                        k = (b + 1) * 3 + (c + 1)
                        terms[b, c] = (
                            weights[k, x] * source[-1]
                            + weights[9 + k, x] * source[0]
                            + weights[18 + k, x] * source[1]
                        )
                image[j, x] = spread(terms)
                place = inner * 32 + 1 + x
                here = lane == place
                high = jnp.where(here, pltpu.roll(source[0], (place + 1) % 128, 1), high)
                low = jnp.where(here, pltpu.roll(source[0], place % 128, 1), low)
            z_high[group] = high
            z_low[group] = low
        return carry

    lax.fori_loop(0, 16, plane, 0)


def x_faces(krylov, y_low, y_high, after, low, high):
    del after
    for out, x in ((low, 0), (high, 15)):
        out[0:128, :] = krylov[:, x].reshape(128, 128)
        for side, face in ((0, y_low), (1, y_high)):
            for slot in range(4):
                out[pl.ds(128 + slot * 8 + side * 4, 4), :] = face[pl.ds(slot, 4, stride=4), x, :]


def same_row():
    return (lanes((8, 256)) % 8 == rows((8, 256))).astype(F32)


def fold_rows(product):
    groups = product.shape[0] // 8
    return jnp.sum(product.reshape(groups, 8, 256) * same_row()[None], axis=1)


def fold_lanes(value):
    value = value + roll(value, 127, 1)
    value = value + roll(value, 126, 1)
    value = value + roll(value, 124, 1)
    return jnp.where(lanes(value.shape) % 8 == 0, value, 0.0)


def pack(value):
    total = None
    for group in range(value.shape[0] // 8):
        for half in range(2):
            part = fold_lanes(value[group * 8 : group * 8 + 8, half * 128 : half * 128 + 128])
            part = roll(part, group * 2 + half, 1)
            total = part if total is None else total + part
    return total


def unpack(value, groups):
    out = []
    lane = lanes(value.shape)
    for group in range(groups):
        halves = []
        for half in range(2):
            part = jnp.where(lane % 8 == 0, roll(value, -(group * 2 + half), 1), 0.0)
            part = part + roll(part, 1, 1)
            part = part + roll(part, 2, 1)
            halves.append(part + roll(part, 4, 1))
        out.append(jnp.concatenate(halves, axis=1))
    return jnp.concatenate(out, axis=0)


def basis_kernel(scale, basis, y_low, y_high, flat, gram, edge_basis, edge_y):
    for x in range(16):
        block = basis[:, x].astype(F32).reshape(256, 128)
        flat[:, x * 128 : x * 128 + 128] = block.astype(BF16)
    whole = flat[...]
    product = lax.dot_general(whole, whole, NT, preferred_element_type=F32)
    gram[...] = pack(fold_rows(product)) * scale
    row = rows((2048, 128))
    lane = lanes((2048, 128))
    x = row // 128
    z = row % 128
    chosen = jnp.where(((z == 0) & (lane == 1 + x)) | ((z == 127) & (lane == 65 + x)), 1.0, 0.0)
    edge_basis[...] = jnp.dot(
        whole, chosen.astype(BF16), preferred_element_type=F32
    ).astype(BF16)
    line = lanes((16, 128))
    columns = jnp.zeros((16, 128), F32)
    for yside, face in ((0, y_low), (1, y_high)):
        for j in range(16):
            place = (j % 4) * 8 + yside * 4 + j // 4
            columns = jnp.where(line == place, roll(face[j], place + 1, 1), columns)
            columns = jnp.where(line == 64 + place, roll(face[j], 64 + place, 1), columns)
    turned = jnp.concatenate([columns, jnp.zeros((112, 128), F32)], axis=0).T
    lane = lanes((8, 128))
    for side in range(2):
        total = jnp.zeros((8, 128), F32)
        for slot in range(4):
            part = turned[side * 64 + slot * 8 : side * 64 + slot * 8 + 8, :]
            inside = (lane >= slot * 32 + 1) & (lane < slot * 32 + 17)
            total = jnp.where(inside, roll(part, slot * 32 + 1, 1), total)
        edge_y[side] = total


def z_faces(z_high, z_low, edge_y, x_low, x_high, out_high, out_low):
    lane = lanes((8, 128))
    for side, (own, out) in enumerate(((z_high, out_high), (z_low, out_low))):
        for group in range(5):
            value = edge_y[side] if group == 4 else own[group]
            for slot in range(4):
                first = 128 + slot * 8 if group == 4 else (group * 4 + slot) * 8
                for face, q in ((x_low, 0), (x_high, 17)):
                    place = slot * 32 + q
                    part = roll(face[first : first + 8, :], place + 1 - side, 1)
                    value = jnp.where(lane == place, part, value)
            out[group * 8 : group * 8 + 8, :] = value


def corrections(y_low, y_high, x_low, x_high, face_x, face_y, flat, given, image, partial, halves):
    row = rows((16, 128))

    def vector(j, carry):
        for side, (face, x) in enumerate(((x_low, 0), (x_high, 15))):
            source = face[pl.ds(pl.multiple_of(j * 8, 8), 8), :]
            terms = {}
            for b in STEPS:
                for c in STEPS:
                    terms[b, c] = face_x[side, (b + 1) * 3 + c + 1] * source
            image[j, x] = given[j, x] + spread(terms)
        for x in range(1, 15):
            image[j, x] = given[j, x]
        corner = 128 + (j % 4) * 8 + j // 4
        for side, (face, y) in enumerate(((y_low, 0), (y_high, 7))):
            middle = face[j]
            before = jnp.where(row == 0, x_low[pl.ds(corner + side * 4, 1), :], roll(middle, 1, 0))
            after = jnp.where(row == 15, x_high[pl.ds(corner + side * 4, 1), :], roll(middle, -1, 0))
            total = None
            for c in STEPS:
                part = (
                    face_y[side, c + 1] * before
                    + face_y[side, 3 + c + 1] * middle
                    + face_y[side, 6 + c + 1] * after
                )
                part = roll(part, -c, 1)
                total = part if total is None else total + part
            image[j, :, y, :] = image[j, :, y, :] + total
        return carry

    lax.fori_loop(0, 16, vector, 0)
    for x in range(16):
        block = image[:, x].reshape(128, 128)
        upper = block.astype(BF16)
        halves[0:128, x * 128 : x * 128 + 128] = upper
        halves[128:256, x * 128 : x * 128 + 128] = (block - upper.astype(F32)).astype(BF16)
    product = lax.dot_general(halves[...], flat[...], NT, preferred_element_type=F32)
    partial[...] = fold_rows(product[0:128] + product[128:256])


def finish(scale, from_low, from_high, face_z, edge_basis, partial, gram, columns, payload):
    row = rows((8, 128))
    lane = lanes((8, 128))
    for j in range(16):
        columns[j * 8 : j * 8 + 8, :] = jnp.zeros((8, 128), F32)
    for side, received in enumerate((from_low, from_high)):
        totals = [None] * 4
        for a in STEPS:
            edge = roll(received[32:40, :], -a, 1)
            for group in range(4):
                middle = roll(received[group * 8 : group * 8 + 8, :], -a, 1)
                below = jnp.where(row == 0, edge[group : group + 1, :], roll(middle, 1, 0))
                above = jnp.where(row == 7, edge[4 + group : 5 + group, :], roll(middle, -1, 0))
                k = (a + 1) * 3
                part = (
                    face_z[side, k] * below
                    + face_z[side, k + 1] * middle
                    + face_z[side, k + 2] * above
                )
                totals[group] = part if totals[group] is None else totals[group] + part
        for group in range(4):
            for slot in range(4):
                j = group * 4 + slot
                inside = (lane >= side * 64) & (lane < side * 64 + 32)
                part = roll(totals[group], side * 64 - slot * 32, 1)
                columns[j * 8 : j * 8 + 8, :] += jnp.where(inside, part, 0.0)
    value = columns[...]
    upper = value.astype(BF16)
    lower = (value - upper.astype(F32)).astype(BF16)
    both = jnp.concatenate([upper, lower], axis=0)
    product = lax.dot_general(both, edge_basis[...], NT, preferred_element_type=F32)
    first = partial[...] + fold_rows(product[0:128] + product[128:256])
    payload[0:8, :] = pack(first) * scale
    payload[8:16, :] = gram[...]


def project(parts, given, columns, flat, image, coefficients):
    total = parts[0]
    for k in range(1, parts.shape[0]):
        total = total + parts[k]
    first = unpack(total[0:8], 2)
    gram = unpack(total[8:16], 4)
    applied = jnp.zeros((16, 256), F32)
    for i in range(32):
        applied = applied + first[:, i * 8 : i * 8 + 1] * gram[i : i + 1, :]
    both = first + (first - applied)
    pick = (lanes((32, 256)) == 8 * rows((32, 256))).astype(F32)
    coefficients[...] = lax.dot_general(
        pick, both, NT, precision=lax.Precision.HIGHEST, preferred_element_type=F32
    )
    wide = (both.reshape(16, 1, 256) * same_row()[None]).reshape(128, 256)
    upper = wide.astype(BF16)
    lower = (wide - upper.astype(F32)).astype(BF16)
    left = jnp.concatenate([upper, lower], axis=0)
    lane = lanes((128, 128))
    column = columns[...]
    for x in range(16):
        product = jnp.dot(left, flat[:, x * 128 : x * 128 + 128], preferred_element_type=F32)
        block = given[:, x].reshape(128, 128)
        block = block + jnp.where(lane == 0, roll(column, -(1 + x), 1), 0.0)
        block = block + jnp.where(lane == 127, roll(column, 62 - x, 1), 0.0)
        block = block - (product[0:128] + product[128:256])
        image[:, x] = block.reshape(16, 8, 128)


def shifted(low_out, high_out, axis):
    count = lax.axis_size(axis)
    forward = [(i, i + 1) for i in range(count - 1)]
    backward = [(target, source) for source, target in forward]
    return lax.ppermute(high_out, axis, forward), lax.ppermute(low_out, axis, backward)


def summed(values, axis, last=False):
    copies = jnp.broadcast_to(values[None], (lax.axis_size(axis),) + values.shape)
    parts = lax.all_to_all(copies, axis, 0, 0)
    return parts if last else parts.sum(0)


def local(basis, krylov, center, couplings):
    cells = krylov[0].size * lax.axis_size("gx") * lax.axis_size("gy") * lax.axis_size("gz")
    scale = 1.0 / cells
    face = like((16, 16, 128))
    low, high = call("y_faces", y_faces, (face, face), data=1 << 20)(krylov)
    y_low, y_high = shifted(low, high, "gy")
    small = like((4, 8, 128))
    image, z_high, z_low, face_x, face_y, face_z = call(
        "interior",
        interior,
        (
            like((16, 16, 8, 128)),
            small,
            small,
            like((2, 9, 8, 128)),
            like((2, 9, 16, 128)),
            like((2, 9, 8, 128)),
        ),
        scratch=[pltpu.VMEM((27, 16, 8, 128), F32), pltpu.VMEM((18, 16, 8, 128), F32)],
        flops=1 << 24,
        data=4 << 20,
    )(krylov, center, couplings)
    side = like((160, 128))
    low, high = call("x_faces", x_faces, (side, side), data=1 << 20)(krylov, y_low, y_high, z_high)
    x_low, x_high = shifted(low, high, "gx")
    flat, gram, edge_basis, edge_y = call(
        "basis",
        lambda *refs: basis_kernel(scale, *refs),
        (
            like((256, 2048), BF16),
            like((8, 128)),
            like((256, 128), BF16),
            like((2, 8, 128)),
        ),
        flops=1 << 28,
        data=2 << 20,
    )(basis, y_low, y_high)
    end = like((40, 128))
    high, low = call("z_faces", z_faces, (end, end), data=1 << 18)(z_high, z_low, edge_y, x_low, x_high)
    from_low, from_high = shifted(low, high, "gz")
    image, partial = call(
        "corrections",
        corrections,
        (like((16, 16, 8, 128)), like((16, 256))),
        scratch=[pltpu.VMEM((256, 2048), BF16)],
        flops=1 << 28,
        data=4 << 20,
    )(y_low, y_high, x_low, x_high, face_x, face_y, flat, image)
    columns, payload = call(
        "finish",
        lambda *refs: finish(scale, *refs),
        (like((128, 128)), like((16, 128))),
        data=1 << 18,
    )(from_low, from_high, face_z, edge_basis, partial, gram)
    payload = summed(payload, "gz")
    payload = summed(payload, "gx")
    parts = summed(payload, "gy", last=True)
    projected, coefficients = call(
        "project",
        project,
        (like((16, 16, 8, 128)), like((32, 16))),
        flops=1 << 28,
        data=3 << 20,
    )(parts, image, columns, flat)
    return projected, coefficients


def solution(mesh):
    in_specs = (
        P(None, "gx", "gy", "gz"),
        P(None, "gx", "gy", "gz"),
        P("gx", "gy", "gz"),
        P(None, "gx", "gy", "gz"),
    )
    out_specs = (P(None, "gx", "gy", "gz"), P())
    return jax.shard_map(local, mesh=mesh, in_specs=in_specs, out_specs=out_specs, check_vma=False)
```

```python
import jax
import jax.numpy as jnp
import numpy as np
from jax import lax
from jax.experimental import pallas as pl
from jax.experimental.pallas import tpu as pltpu
from jax.sharding import PartitionSpec as P

F32 = jnp.float32
BF16 = jnp.bfloat16
NT = (((1,), (1,)), ((), ()))
STEPS = (-1, 0, 1)


def call(name, body, out, scratch=(), flops=0, data=0, specs=None):
    single = not isinstance(out, (tuple, list))
    shapes = (out,) if single else tuple(out)
    built = pl.pallas_call(
        body,
        name=name,
        out_shape=shapes[0] if single else shapes,
        scratch_shapes=list(scratch),
        **(specs or {}),
        compiler_params=pltpu.CompilerParams(vmem_limit_bytes=16 << 20),
        cost_estimate=pl.CostEstimate(flops=flops, bytes_accessed=data, transcendentals=0),
    )
    return built


def like(shape, dtype=F32):
    return jax.ShapeDtypeStruct(shape, dtype)


def roll(value, shift, axis):
    size = value.shape[axis]
    shift = shift % size
    return value if shift == 0 else pltpu.roll(value, shift, axis)


def lanes(shape):
    return lax.broadcasted_iota(jnp.int32, shape, len(shape) - 1)


def rows(shape):
    return lax.broadcasted_iota(jnp.int32, shape, len(shape) - 2)


def spread(terms):
    total = None
    for c in STEPS:
        part = terms[0, c] + roll(terms[-1, c], 1, 0) + roll(terms[1, c], -1, 0)
        part = roll(part, -c, 1)
        total = part if total is None else total + part
    return total


def y_faces(krylov, low, high, done):
    copies = [
        pltpu.make_async_copy(krylov.at[:, :, y, :], out, done.at[k])
        for k, (out, y) in enumerate(((low, 0), (high, 7)))
    ]
    for copy in copies:
        copy.start()
    for copy in copies:
        copy.wait()


def number(a, b, c):
    k = (a + 1) * 9 + (b + 1) * 3 + (c + 1)
    return k if k < 13 else k - 1


def interior(krylov, center, couplings, image, z_high, z_low, face_x, face_y, face_z, weights, flat):
    lane = lanes((8, 128))
    row = rows((8, 128))
    slot = lanes((8, 128)) % 32

    def prepare(x, carry):
        edge_of = {}
        for a in STEPS:
            for b in STEPS:
                for c in STEPS:
                    index = (a + 1) * 9 + (b + 1) * 3 + (c + 1)
                    if (a, b, c) == (0, 0, 0):
                        value = center[x].astype(F32)
                    else:
                        value = couplings[number(a, b, c), x].astype(F32)
                    edge_of[a, b, c] = value
                    if c == -1:
                        value = jnp.where(lane == 0, 0.0, value)
                    if c == 1:
                        value = jnp.where(lane == 127, 0.0, value)
                    value = roll(value, c, 1)
                    if b != 0:
                        flat[(a + 1) * 6 + (b + 1) // 2 * 3 + (c + 1), x] = value
                        value = jnp.where(row == (0 if b == -1 else 7), 0.0, value)
                    value = roll(value, b, 0)
                    weights[index, x] = value
        for a in STEPS:
            for b in STEPS:
                both = jnp.where(lane == 127, edge_of[a, b, 1], edge_of[a, b, -1])
                for side, start in ((0, 0), (1, 127)):
                    moved = pltpu.roll(both, (x + 1 + 128 - start) % 128, 1)
                    k = (a + 1) * 3 + b + 1
                    face_z[side, k] = jnp.where(lane == x + 1, moved, face_z[side, k])
        return carry

    face_z[...] = jnp.zeros_like(face_z)
    lax.fori_loop(0, 16, prepare, 0)
    for side in range(2):
        for k in range(9):
            value = face_z[side, k]
            value = value + roll(value, 32, 1)
            face_z[side, k] = value + roll(value, 64, 1)
    zero = jnp.zeros((8, 128), F32)
    for k in range(9):
        face_x[0, k] = weights[k, 0]
        face_x[1, k] = weights[18 + k, 15]
        weights[k, 0] = zero
        weights[18 + k, 15] = zero
    for a in range(3):
        for c in range(3):
            face_y[0, a * 3 + c] = flat[a * 6 + c, :, 0, :]
            face_y[1, a * 3 + c] = flat[a * 6 + 3 + c, :, 7, :]

    z_high[...] = jnp.zeros_like(z_high)
    z_low[...] = jnp.zeros_like(z_low)

    def plane(x, carry):
        before = jnp.maximum(x - 1, 0)
        after = jnp.minimum(x + 1, 15)
        for group in range(4):
            high = z_high[group]
            low = z_low[group]
            for inner in range(4):
                j = group * 4 + inner
                source = {-1: krylov[j, before], 0: krylov[j, x], 1: krylov[j, after]}
                terms = {}
                for b in STEPS:
                    for c in STEPS:
                        k = (b + 1) * 3 + (c + 1)
                        terms[b, c] = (
                            weights[k, x] * source[-1]
                            + weights[9 + k, x] * source[0]
                            + weights[18 + k, x] * source[1]
                        )
                image[j, x] = spread(terms)
                place = inner * 32 + 1 + x
                here = lane == place
                high = jnp.where(here, pltpu.roll(source[0], (place + 1) % 128, 1), high)
                low = jnp.where(here, pltpu.roll(source[0], place % 128, 1), low)
            z_high[group] = high
            z_low[group] = low
        return carry

    lax.fori_loop(0, 16, plane, 0)


def x_faces(krylov, y_low, y_high, after, low, high):
    del after
    for out, x in ((low, 0), (high, 15)):
        out[0:128, :] = krylov[:, x].reshape(128, 128)
        for side, face in ((0, y_low), (1, y_high)):
            for slot in range(4):
                out[pl.ds(128 + slot * 8 + side * 4, 4), :] = face[pl.ds(slot, 4, stride=4), x, :]


def same_row():
    return (lanes((8, 256)) % 8 == rows((8, 256))).astype(F32)


def fold_rows(product):
    groups = product.shape[0] // 8
    return jnp.sum(product.reshape(groups, 8, 256) * same_row()[None], axis=1)


def fold_lanes(value):
    value = value + roll(value, 127, 1)
    value = value + roll(value, 126, 1)
    value = value + roll(value, 124, 1)
    return jnp.where(lanes(value.shape) % 8 == 0, value, 0.0)


def pack(value):
    total = None
    for group in range(value.shape[0] // 8):
        for half in range(2):
            part = fold_lanes(value[group * 8 : group * 8 + 8, half * 128 : half * 128 + 128])
            part = roll(part, group * 2 + half, 1)
            total = part if total is None else total + part
    return total


def unpack(value, groups):
    out = []
    lane = lanes(value.shape)
    for group in range(groups):
        halves = []
        for half in range(2):
            part = jnp.where(lane % 8 == 0, roll(value, -(group * 2 + half), 1), 0.0)
            part = part + roll(part, 1, 1)
            part = part + roll(part, 2, 1)
            halves.append(part + roll(part, 4, 1))
        out.append(jnp.concatenate(halves, axis=1))
    return jnp.concatenate(out, axis=0)


def basis_kernel(scale, basis, y_low, y_high, flat, gram, edge_basis, edge_y):
    for x in range(16):
        block = basis[:, x].astype(F32).reshape(256, 128)
        flat[:, x * 128 : x * 128 + 128] = block.astype(BF16)
    whole = flat[...]
    product = lax.dot_general(whole, whole, NT, preferred_element_type=F32)
    gram[...] = pack(fold_rows(product)) * scale
    row = rows((2048, 128))
    lane = lanes((2048, 128))
    x = row // 128
    z = row % 128
    chosen = jnp.where(((z == 0) & (lane == 1 + x)) | ((z == 127) & (lane == 65 + x)), 1.0, 0.0)
    edge_basis[...] = jnp.dot(
        whole, chosen.astype(BF16), preferred_element_type=F32
    ).astype(BF16)
    line = lanes((16, 128))
    columns = jnp.zeros((16, 128), F32)
    for yside, face in ((0, y_low), (1, y_high)):
        for j in range(16):
            place = (j % 4) * 8 + yside * 4 + j // 4
            columns = jnp.where(line == place, roll(face[j], place + 1, 1), columns)
            columns = jnp.where(line == 64 + place, roll(face[j], 64 + place, 1), columns)
    turned = jnp.concatenate([columns, jnp.zeros((112, 128), F32)], axis=0).T
    lane = lanes((8, 128))
    for side in range(2):
        total = jnp.zeros((8, 128), F32)
        for slot in range(4):
            part = turned[side * 64 + slot * 8 : side * 64 + slot * 8 + 8, :]
            inside = (lane >= slot * 32 + 1) & (lane < slot * 32 + 17)
            total = jnp.where(inside, roll(part, slot * 32 + 1, 1), total)
        edge_y[side] = total


def z_faces(odd, z_high, z_low, edge_y, x_low, x_high, near, far):
    lane = lanes((8, 128))
    values = []
    for side, own in enumerate((z_high, z_low)):
        for group in range(5):
            value = edge_y[side] if group == 4 else own[group]
            for slot in range(4):
                first = 128 + slot * 8 if group == 4 else (group * 4 + slot) * 8
                for face, q in ((x_low, 0), (x_high, 17)):
                    place = slot * 32 + q
                    part = roll(face[first : first + 8, :], place + 1 - side, 1)
                    value = jnp.where(lane == place, part, value)
            values.append(value)
    flipped = odd[0] == 1
    for group in range(5):
        high, low = values[group], values[5 + group]
        near[group * 8 : group * 8 + 8, :] = jnp.where(flipped, low, high)
        far[group * 8 : group * 8 + 8, :] = jnp.where(flipped, high, low)


def corrections(y_low, y_high, x_low, x_high, face_x, face_y, flat, given, image, partial, halves):
    row = rows((16, 128))

    def vector(j, carry):
        for side, (face, x) in enumerate(((x_low, 0), (x_high, 15))):
            source = face[pl.ds(pl.multiple_of(j * 8, 8), 8), :]
            terms = {}
            for b in STEPS:
                for c in STEPS:
                    terms[b, c] = face_x[side, (b + 1) * 3 + c + 1] * source
            image[j, x] = given[j, x] + spread(terms)
        for x in range(1, 15):
            image[j, x] = given[j, x]
        corner = 128 + (j % 4) * 8 + j // 4
        for side, (face, y) in enumerate(((y_low, 0), (y_high, 7))):
            middle = face[j]
            before = jnp.where(row == 0, x_low[pl.ds(corner + side * 4, 1), :], roll(middle, 1, 0))
            after = jnp.where(row == 15, x_high[pl.ds(corner + side * 4, 1), :], roll(middle, -1, 0))
            total = None
            for c in STEPS:
                part = (
                    face_y[side, c + 1] * before
                    + face_y[side, 3 + c + 1] * middle
                    + face_y[side, 6 + c + 1] * after
                )
                part = roll(part, -c, 1)
                total = part if total is None else total + part
            image[j, :, y, :] = image[j, :, y, :] + total
        return carry

    lax.fori_loop(0, 16, vector, 0)
    for x in range(16):
        block = image[:, x].reshape(128, 128)
        upper = block.astype(BF16)
        halves[0:128, x * 128 : x * 128 + 128] = upper
        halves[128:256, x * 128 : x * 128 + 128] = (block - upper.astype(F32)).astype(BF16)
    product = lax.dot_general(halves[...], flat[...], NT, preferred_element_type=F32)
    partial[...] = fold_rows(product[0:128] + product[128:256])


def finish(scale, odd, near, far, face_z, edge_basis, partial, gram, columns, payload):
    row = rows((8, 128))
    lane = lanes((8, 128))
    for j in range(16):
        columns[j * 8 : j * 8 + 8, :] = jnp.zeros((8, 128), F32)
    flipped = odd[0] == 1
    for side in range(2):
        pair = (far, near) if side == 0 else (near, far)
        received = jnp.where(flipped, pair[1][...], pair[0][...])
        totals = [None] * 4
        for a in STEPS:
            edge = roll(received[32:40, :], -a, 1)
            for group in range(4):
                middle = roll(received[group * 8 : group * 8 + 8, :], -a, 1)
                below = jnp.where(row == 0, edge[group : group + 1, :], roll(middle, 1, 0))
                above = jnp.where(row == 7, edge[4 + group : 5 + group, :], roll(middle, -1, 0))
                k = (a + 1) * 3
                part = (
                    face_z[side, k] * below
                    + face_z[side, k + 1] * middle
                    + face_z[side, k + 2] * above
                )
                totals[group] = part if totals[group] is None else totals[group] + part
        for group in range(4):
            for slot in range(4):
                j = group * 4 + slot
                inside = (lane >= side * 64) & (lane < side * 64 + 32)
                part = roll(totals[group], side * 64 - slot * 32, 1)
                columns[j * 8 : j * 8 + 8, :] += jnp.where(inside, part, 0.0)
    value = columns[...]
    upper = value.astype(BF16)
    lower = (value - upper.astype(F32)).astype(BF16)
    both = jnp.concatenate([upper, lower], axis=0)
    product = lax.dot_general(both, edge_basis[...], NT, preferred_element_type=F32)
    first = partial[...] + fold_rows(product[0:128] + product[128:256])
    payload[0:8, :] = pack(first) * scale
    payload[8:16, :] = gram[...]


def project(parts, given, columns, flat, image, coefficients, ready, done):
    total = parts[0]
    for k in range(1, parts.shape[0]):
        total = total + parts[k]
    first = unpack(total[0:8], 2)
    gram = unpack(total[8:16], 4)
    applied = jnp.zeros((16, 256), F32)
    for i in range(32):
        applied = applied + first[:, i * 8 : i * 8 + 1] * gram[i : i + 1, :]
    both = first + (first - applied)
    pick = (lanes((32, 256)) == 8 * rows((32, 256))).astype(F32)
    coefficients[...] = lax.dot_general(
        both, pick, NT, precision=lax.Precision.HIGHEST, preferred_element_type=F32
    )
    wide = (both.reshape(16, 1, 256) * same_row()[None]).reshape(128, 256)
    upper = wide.astype(BF16)
    lower = (wide - upper.astype(F32)).astype(BF16)
    left = jnp.concatenate([upper, lower], axis=0)
    lane = lanes((128, 128))
    column = columns[...]
    above = roll(column, -65, 1)
    mixed = [jnp.where(lane % 2 == 1 - k, column, above) for k in range(2)]
    ends = (lane == 0) | (lane == 127)
    copies = []
    for pair in range(8):
        product = jnp.dot(left, flat[:, pair * 256 : pair * 256 + 256], preferred_element_type=F32)
        product = product[0:128] + product[128:256]
        for inner in range(2):
            x = pair * 2 + inner
            block = given[:, x].reshape(128, 128)
            block = block + jnp.where(ends, roll(mixed[x % 2], -(1 + x), 1), 0.0)
            block = block - product[:, inner * 128 : inner * 128 + 128]
            ready[:, x] = block.reshape(16, 8, 128)
        span = pl.ds(pair * 2, 2)
        copies.append(pltpu.make_async_copy(ready.at[:, span], image.at[:, span], done.at[pair]))
        copies[-1].start()
    for copy in copies:
        copy.wait()


def shifted(low_out, high_out, axis):
    count = lax.axis_size(axis)
    forward = [(i, i + 1) for i in range(count - 1)]
    backward = [(target, source) for source, target in forward]
    return lax.ppermute(high_out, axis, forward), lax.ppermute(low_out, axis, backward)


def summed(values, axis, last=False):
    copies = jnp.broadcast_to(values[None], (lax.axis_size(axis),) + values.shape)
    parts = lax.all_to_all(copies, axis, 0, 0)
    return parts if last else parts.sum(0)


def local(basis, krylov, center, couplings):
    cells = krylov[0].size * lax.axis_size("gx") * lax.axis_size("gy") * lax.axis_size("gz")
    scale = 1.0 / cells
    face = like((16, 16, 128))
    low, high = call(
        "y_faces",
        y_faces,
        (face, face),
        scratch=[pltpu.SemaphoreType.DMA((2,))],
        data=1 << 18,
        specs={"in_specs": [pl.BlockSpec(memory_space=pltpu.HBM)]},
    )(pltpu.with_memory_space_constraint(krylov, pltpu.HBM))
    y_low, y_high = shifted(low, high, "gy")
    small = like((4, 8, 128))
    image, z_high, z_low, face_x, face_y, face_z = call(
        "interior",
        interior,
        (
            like((16, 16, 8, 128)),
            small,
            small,
            like((2, 9, 8, 128)),
            like((2, 9, 16, 128)),
            like((2, 9, 8, 128)),
        ),
        scratch=[pltpu.VMEM((27, 16, 8, 128), F32), pltpu.VMEM((18, 16, 8, 128), F32)],
        flops=1 << 24,
        data=4 << 20,
    )(krylov, center, couplings)
    side = like((160, 128))
    low, high = call("x_faces", x_faces, (side, side), data=1 << 20)(krylov, y_low, y_high, z_high)
    x_low, x_high = shifted(low, high, "gx")
    flat, gram, edge_basis, edge_y = call(
        "basis",
        lambda *refs: basis_kernel(scale, *refs),
        (
            like((256, 2048), BF16),
            like((8, 128)),
            like((256, 128), BF16),
            like((2, 8, 128)),
        ),
        flops=1 << 28,
        data=2 << 20,
    )(basis, y_low, y_high)
    end = like((40, 128))
    odd = jnp.bitwise_and(lax.axis_index("gz"), 1).astype(jnp.int32).reshape(1)
    scalar = pl.BlockSpec(memory_space=pltpu.SMEM)
    block = pl.BlockSpec()
    near, far = call(
        "z_faces", z_faces, (end, end), data=1 << 18, specs={"in_specs": [scalar] + [block] * 5}
    )(odd, z_high, z_low, edge_y, x_low, x_high)
    count = lax.axis_size("gz")
    near = lax.ppermute(near, "gz", [(i, i ^ 1) for i in range(count)])
    inner = range(1, count - 1)
    far = lax.ppermute(far, "gz", [(i, ((i + 1) ^ 1) - 1) for i in inner])
    image, partial = call(
        "corrections",
        corrections,
        (like((16, 16, 8, 128)), like((16, 256))),
        scratch=[pltpu.VMEM((256, 2048), BF16)],
        flops=1 << 28,
        data=4 << 20,
    )(y_low, y_high, x_low, x_high, face_x, face_y, flat, image)
    columns, payload = call(
        "finish",
        lambda *refs: finish(scale, *refs),
        (like((128, 128)), like((16, 128))),
        data=1 << 18,
        specs={"in_specs": [scalar] + [block] * 6},
    )(odd, near, far, face_z, edge_basis, partial, gram)
    payload = summed(payload, "gz")
    payload = summed(payload, "gx")
    parts = summed(payload, "gy", last=True)
    projected, coefficients = call(
        "project",
        project,
        (like((16, 16, 8, 128)), like((16, 32))),
        scratch=[pltpu.VMEM((16, 16, 8, 128), F32), pltpu.SemaphoreType.DMA((8,))],
        flops=1 << 28,
        data=3 << 20,
        specs={
            "out_specs": (
                pl.BlockSpec(memory_space=pl.ANY),
                pl.BlockSpec(memory_space=pltpu.VMEM),
            )
        },
    )(parts, image, columns, flat)
    return projected, coefficients.T


def solution(mesh):
    in_specs = (
        P(None, "gx", "gy", "gz"),
        P(None, "gx", "gy", "gz"),
        P("gx", "gy", "gz"),
        P(None, "gx", "gy", "gz"),
    )
    out_specs = (P(None, "gx", "gy", "gz"), P())
    return jax.shard_map(local, mesh=mesh, in_specs=in_specs, out_specs=out_specs, check_vma=False)
```

```python
import jax
import jax.numpy as jnp
import numpy as np
from jax import lax
from jax.experimental import pallas as pl
from jax.experimental.pallas import tpu as pltpu
from jax.sharding import PartitionSpec as P

F32 = jnp.float32
BF16 = jnp.bfloat16
NT = (((1,), (1,)), ((), ()))
STEPS = (-1, 0, 1)


def call(name, body, out, scratch=(), flops=0, data=0, specs=None):
    single = not isinstance(out, (tuple, list))
    shapes = (out,) if single else tuple(out)
    built = pl.pallas_call(
        body,
        name=name,
        out_shape=shapes[0] if single else shapes,
        scratch_shapes=list(scratch),
        **(specs or {}),
        compiler_params=pltpu.CompilerParams(vmem_limit_bytes=40 << 20),
        cost_estimate=pl.CostEstimate(flops=flops, bytes_accessed=data, transcendentals=0),
    )
    return built


def like(shape, dtype=F32):
    return jax.ShapeDtypeStruct(shape, dtype)


def roll(value, shift, axis):
    size = value.shape[axis]
    shift = shift % size
    return value if shift == 0 else pltpu.roll(value, shift, axis)


def lanes(shape):
    return lax.broadcasted_iota(jnp.int32, shape, len(shape) - 1)


def rows(shape):
    return lax.broadcasted_iota(jnp.int32, shape, len(shape) - 2)


def spread(terms):
    total = None
    for c in STEPS:
        part = terms[0, c] + roll(terms[-1, c], 1, 0) + roll(terms[1, c], -1, 0)
        part = roll(part, -c, 1)
        total = part if total is None else total + part
    return total


def y_faces(krylov, low, high):
    low[...] = krylov[:, :, 0, :]
    high[...] = krylov[:, :, 7, :]


def number(a, b, c):
    k = (a + 1) * 9 + (b + 1) * 3 + (c + 1)
    return k if k < 13 else k - 1


def interior(krylov, center, couplings, image, z_high, z_low, face_x, face_y, face_z, weights, flat):
    lane = lanes((8, 128))
    row = rows((8, 128))
    slot = lanes((8, 128)) % 32

    def prepare(x, carry):
        edge_of = {}
        for a in STEPS:
            for b in STEPS:
                for c in STEPS:
                    index = (a + 1) * 9 + (b + 1) * 3 + (c + 1)
                    if (a, b, c) == (0, 0, 0):
                        value = center[x].astype(F32)
                    else:
                        value = couplings[number(a, b, c), x].astype(F32)
                    edge_of[a, b, c] = value
                    if c == -1:
                        value = jnp.where(lane == 0, 0.0, value)
                    if c == 1:
                        value = jnp.where(lane == 127, 0.0, value)
                    value = roll(value, c, 1)
                    if b != 0:
                        flat[(a + 1) * 6 + (b + 1) // 2 * 3 + (c + 1), x] = value
                        value = jnp.where(row == (0 if b == -1 else 7), 0.0, value)
                    value = roll(value, b, 0)
                    weights[index, x] = value
        for a in STEPS:
            for b in STEPS:
                both = jnp.where(lane == 127, edge_of[a, b, 1], edge_of[a, b, -1])
                for side, start in ((0, 0), (1, 127)):
                    moved = pltpu.roll(both, (x + 1 + 128 - start) % 128, 1)
                    k = (a + 1) * 3 + b + 1
                    face_z[side, k] = jnp.where(lane == x + 1, moved, face_z[side, k])
        return carry

    face_z[...] = jnp.zeros_like(face_z)
    lax.fori_loop(0, 16, prepare, 0)
    for side in range(2):
        for k in range(9):
            value = face_z[side, k]
            value = value + roll(value, 32, 1)
            face_z[side, k] = value + roll(value, 64, 1)
    zero = jnp.zeros((8, 128), F32)
    for k in range(9):
        face_x[0, k] = weights[k, 0]
        face_x[1, k] = weights[18 + k, 15]
        weights[k, 0] = zero
        weights[18 + k, 15] = zero
    for a in range(3):
        for c in range(3):
            face_y[0, a * 3 + c] = flat[a * 6 + c, :, 0, :]
            face_y[1, a * 3 + c] = flat[a * 6 + 3 + c, :, 7, :]

    z_high[...] = jnp.zeros_like(z_high)
    z_low[...] = jnp.zeros_like(z_low)

    def plane(x, carry):
        before = jnp.maximum(x - 1, 0)
        after = jnp.minimum(x + 1, 15)
        for group in range(4):
            high = z_high[group]
            low = z_low[group]
            for inner in range(4):
                j = group * 4 + inner
                source = {-1: krylov[j, before], 0: krylov[j, x], 1: krylov[j, after]}
                terms = {}
                for b in STEPS:
                    for c in STEPS:
                        k = (b + 1) * 3 + (c + 1)
                        terms[b, c] = (
                            weights[k, x] * source[-1]
                            + weights[9 + k, x] * source[0]
                            + weights[18 + k, x] * source[1]
                        )
                image[j, x] = spread(terms)
                place = inner * 32 + 1 + x
                here = lane == place
                high = jnp.where(here, pltpu.roll(source[0], (place + 1) % 128, 1), high)
                low = jnp.where(here, pltpu.roll(source[0], place % 128, 1), low)
            z_high[group] = high
            z_low[group] = low
        return carry

    lax.fori_loop(0, 16, plane, 0)


def x_faces(krylov, y_low, y_high, after, low, high):
    del after
    for out, x in ((low, 0), (high, 15)):
        out[0:128, :] = krylov[:, x].reshape(128, 128)
        for side, face in ((0, y_low), (1, y_high)):
            for slot in range(4):
                out[pl.ds(128 + slot * 8 + side * 4, 4), :] = face[pl.ds(slot, 4, stride=4), x, :]


def same_row():
    return (lanes((8, 256)) % 8 == rows((8, 256))).astype(F32)


def fold_rows(product):
    groups = product.shape[0] // 8
    return jnp.sum(product.reshape(groups, 8, 256) * same_row()[None], axis=1)


def fold_lanes(value):
    value = value + roll(value, 127, 1)
    value = value + roll(value, 126, 1)
    value = value + roll(value, 124, 1)
    return jnp.where(lanes(value.shape) % 8 == 0, value, 0.0)


def pack(value):
    total = None
    for group in range(value.shape[0] // 8):
        for half in range(2):
            part = fold_lanes(value[group * 8 : group * 8 + 8, half * 128 : half * 128 + 128])
            part = roll(part, group * 2 + half, 1)
            total = part if total is None else total + part
    return total


def unpack(value, groups):
    out = []
    lane = lanes(value.shape)
    for group in range(groups):
        halves = []
        for half in range(2):
            part = jnp.where(lane % 8 == 0, roll(value, -(group * 2 + half), 1), 0.0)
            part = part + roll(part, 1, 1)
            part = part + roll(part, 2, 1)
            halves.append(part + roll(part, 4, 1))
        out.append(jnp.concatenate(halves, axis=1))
    return jnp.concatenate(out, axis=0)


def basis_kernel(scale, basis, y_low, y_high, flat, gram, edge_basis, edge_y):
    for x in range(16):
        block = basis[:, x].astype(F32).reshape(256, 128)
        flat[:, x * 128 : x * 128 + 128] = block.astype(BF16)
    whole = flat[...]
    product = lax.dot_general(whole, whole, NT, preferred_element_type=F32)
    gram[...] = pack(fold_rows(product)) * scale
    row = rows((2048, 128))
    lane = lanes((2048, 128))
    x = row // 128
    z = row % 128
    chosen = jnp.where(((z == 0) & (lane == 1 + x)) | ((z == 127) & (lane == 65 + x)), 1.0, 0.0)
    edge_basis[...] = jnp.dot(
        whole, chosen.astype(BF16), preferred_element_type=F32
    ).astype(BF16)
    line = lanes((16, 128))
    columns = jnp.zeros((16, 128), F32)
    for yside, face in ((0, y_low), (1, y_high)):
        for j in range(16):
            place = (j % 4) * 8 + yside * 4 + j // 4
            columns = jnp.where(line == place, roll(face[j], place + 1, 1), columns)
            columns = jnp.where(line == 64 + place, roll(face[j], 64 + place, 1), columns)
    turned = jnp.concatenate([columns, jnp.zeros((112, 128), F32)], axis=0).T
    lane = lanes((8, 128))
    for side in range(2):
        total = jnp.zeros((8, 128), F32)
        for slot in range(4):
            part = turned[side * 64 + slot * 8 : side * 64 + slot * 8 + 8, :]
            inside = (lane >= slot * 32 + 1) & (lane < slot * 32 + 17)
            total = jnp.where(inside, roll(part, slot * 32 + 1, 1), total)
        edge_y[side] = total


def z_faces(z_high, z_low, edge_y, x_low, x_high, near, far):
    lane = lanes((8, 128))
    values = []
    for side, own in enumerate((z_high, z_low)):
        for group in range(5):
            value = edge_y[side] if group == 4 else own[group]
            for slot in range(4):
                first = 128 + slot * 8 if group == 4 else (group * 4 + slot) * 8
                for face, q in ((x_low, 0), (x_high, 17)):
                    place = slot * 32 + q
                    part = roll(face[first : first + 8, :], place + 1 - side, 1)
                    value = jnp.where(lane == place, part, value)
            values.append(value)
    flipped = jnp.bitwise_and(lax.axis_index("gz"), 1) == 1
    for group in range(5):
        high, low = values[group], values[5 + group]
        near[group * 8 : group * 8 + 8, :] = jnp.where(flipped, low, high)
        far[group * 8 : group * 8 + 8, :] = jnp.where(flipped, high, low)


def corrections(y_low, y_high, x_low, x_high, face_x, face_y, flat, given, image, partial, halves):
    row = rows((16, 128))

    def vector(j, carry):
        for side, (face, x) in enumerate(((x_low, 0), (x_high, 15))):
            source = face[pl.ds(pl.multiple_of(j * 8, 8), 8), :]
            terms = {}
            for b in STEPS:
                for c in STEPS:
                    terms[b, c] = face_x[side, (b + 1) * 3 + c + 1] * source
            image[j, x] = given[j, x] + spread(terms)
        for x in range(1, 15):
            image[j, x] = given[j, x]
        corner = 128 + (j % 4) * 8 + j // 4
        for side, (face, y) in enumerate(((y_low, 0), (y_high, 7))):
            middle = face[j]
            before = jnp.where(row == 0, x_low[pl.ds(corner + side * 4, 1), :], roll(middle, 1, 0))
            after = jnp.where(row == 15, x_high[pl.ds(corner + side * 4, 1), :], roll(middle, -1, 0))
            total = None
            for c in STEPS:
                part = (
                    face_y[side, c + 1] * before
                    + face_y[side, 3 + c + 1] * middle
                    + face_y[side, 6 + c + 1] * after
                )
                part = roll(part, -c, 1)
                total = part if total is None else total + part
            image[j, :, y, :] = image[j, :, y, :] + total
        return carry

    lax.fori_loop(0, 16, vector, 0)
    for x in range(16):
        block = image[:, x].reshape(128, 128)
        upper = block.astype(BF16)
        halves[0:128, x * 128 : x * 128 + 128] = upper
        halves[128:256, x * 128 : x * 128 + 128] = (block - upper.astype(F32)).astype(BF16)
    product = lax.dot_general(halves[...], flat[...], NT, preferred_element_type=F32)
    partial[...] = fold_rows(product[0:128] + product[128:256])


def finish(scale, near, far, face_z, edge_basis, partial, gram, columns, payload):
    row = rows((8, 128))
    lane = lanes((8, 128))
    for j in range(16):
        columns[j * 8 : j * 8 + 8, :] = jnp.zeros((8, 128), F32)
    flipped = jnp.bitwise_and(lax.axis_index("gz"), 1) == 1
    for side in range(2):
        pair = (far, near) if side == 0 else (near, far)
        received = jnp.where(flipped, pair[1][...], pair[0][...])
        totals = [None] * 4
        for a in STEPS:
            edge = roll(received[32:40, :], -a, 1)
            for group in range(4):
                middle = roll(received[group * 8 : group * 8 + 8, :], -a, 1)
                below = jnp.where(row == 0, edge[group : group + 1, :], roll(middle, 1, 0))
                above = jnp.where(row == 7, edge[4 + group : 5 + group, :], roll(middle, -1, 0))
                k = (a + 1) * 3
                part = (
                    face_z[side, k] * below
                    + face_z[side, k + 1] * middle
                    + face_z[side, k + 2] * above
                )
                totals[group] = part if totals[group] is None else totals[group] + part
        for group in range(4):
            for slot in range(4):
                j = group * 4 + slot
                inside = (lane >= side * 64) & (lane < side * 64 + 32)
                part = roll(totals[group], side * 64 - slot * 32, 1)
                columns[j * 8 : j * 8 + 8, :] += jnp.where(inside, part, 0.0)
    value = columns[...]
    upper = value.astype(BF16)
    lower = (value - upper.astype(F32)).astype(BF16)
    both = jnp.concatenate([upper, lower], axis=0)
    product = lax.dot_general(both, edge_basis[...], NT, preferred_element_type=F32)
    first = partial[...] + fold_rows(product[0:128] + product[128:256])
    payload[0:8, :] = pack(first) * scale
    payload[8:16, :] = gram[...]


def project(parts, given, columns, flat, image, coefficients, ready, done):
    total = parts[0]
    for k in range(1, parts.shape[0]):
        total = total + parts[k]
    first = unpack(total[0:8], 2)
    gram = unpack(total[8:16], 4)
    applied = jnp.zeros((16, 256), F32)
    for i in range(32):
        applied = applied + first[:, i * 8 : i * 8 + 1] * gram[i : i + 1, :]
    both = first + (first - applied)
    pick = (lanes((32, 256)) == 8 * rows((32, 256))).astype(F32)
    coefficients[...] = lax.dot_general(
        both, pick, NT, precision=lax.Precision.HIGHEST, preferred_element_type=F32
    )
    wide = (both.reshape(16, 1, 256) * same_row()[None]).reshape(128, 256)
    upper = wide.astype(BF16)
    lower = (wide - upper.astype(F32)).astype(BF16)
    left = jnp.concatenate([upper, lower], axis=0)
    lane = lanes((128, 128))
    column = columns[...]
    above = roll(column, -65, 1)
    mixed = [jnp.where(lane % 2 == 1 - k, column, above) for k in range(2)]
    ends = (lane == 0) | (lane == 127)
    copies = []
    for pair in range(8):
        product = jnp.dot(left, flat[:, pair * 256 : pair * 256 + 256], preferred_element_type=F32)
        product = product[0:128] + product[128:256]
        for inner in range(2):
            x = pair * 2 + inner
            block = given[:, x].reshape(128, 128)
            block = block + jnp.where(ends, roll(mixed[x % 2], -(1 + x), 1), 0.0)
            block = block - product[:, inner * 128 : inner * 128 + 128]
            ready[:, x] = block.reshape(16, 8, 128)
        span = pl.ds(pair * 2, 2)
        copies.append(pltpu.make_async_copy(ready.at[:, span], image.at[:, span], done.at[pair]))
        copies[-1].start()
    for copy in copies:
        copy.wait()


def shifted(low_out, high_out, axis):
    count = lax.axis_size(axis)
    forward = [(i, i + 1) for i in range(count - 1)]
    backward = [(target, source) for source, target in forward]
    return lax.ppermute(high_out, axis, forward), lax.ppermute(low_out, axis, backward)


def summed(values, axis, last=False):
    copies = jnp.broadcast_to(values[None], (lax.axis_size(axis),) + values.shape)
    parts = lax.all_to_all(copies, axis, 0, 0)
    return parts if last else parts.sum(0)


def local(basis, krylov, center, couplings):
    cells = krylov[0].size * lax.axis_size("gx") * lax.axis_size("gy") * lax.axis_size("gz")
    scale = 1.0 / cells
    face = like((16, 16, 128))
    low, high = call("y_faces", y_faces, (face, face), data=1 << 20)(krylov)
    y_low, y_high = shifted(low, high, "gy")
    small = like((4, 8, 128))
    image, z_high, z_low, face_x, face_y, face_z = call(
        "interior",
        interior,
        (
            like((16, 16, 8, 128)),
            small,
            small,
            like((2, 9, 8, 128)),
            like((2, 9, 16, 128)),
            like((2, 9, 8, 128)),
        ),
        scratch=[pltpu.VMEM((27, 16, 8, 128), F32), pltpu.VMEM((18, 16, 8, 128), F32)],
        flops=1 << 24,
        data=4 << 20,
    )(krylov, center, couplings)
    side = like((160, 128))
    low, high = call("x_faces", x_faces, (side, side), data=1 << 20)(krylov, y_low, y_high, z_high)
    x_low, x_high = shifted(low, high, "gx")
    flat, gram, edge_basis, edge_y = call(
        "basis",
        lambda *refs: basis_kernel(scale, *refs),
        (
            like((256, 2048), BF16),
            like((8, 128)),
            like((256, 128), BF16),
            like((2, 8, 128)),
        ),
        flops=1 << 28,
        data=2 << 20,
    )(basis, y_low, y_high)
    end = like((40, 128))
    near, far = call("z_faces", z_faces, (end, end), data=1 << 18)(
        z_high, z_low, edge_y, x_low, x_high
    )
    count = lax.axis_size("gz")
    near = lax.ppermute(near, "gz", [(i, i ^ 1) for i in range(count)])
    inner = range(1, count - 1)
    far = lax.ppermute(far, "gz", [(i, ((i + 1) ^ 1) - 1) for i in inner])
    image, partial = call(
        "corrections",
        corrections,
        (like((16, 16, 8, 128)), like((16, 256))),
        scratch=[pltpu.VMEM((256, 2048), BF16)],
        flops=1 << 28,
        data=4 << 20,
    )(y_low, y_high, x_low, x_high, face_x, face_y, flat, image)
    columns, payload = call(
        "finish",
        lambda *refs: finish(scale, *refs),
        (like((128, 128)), like((16, 128))),
        data=1 << 18,
    )(near, far, face_z, edge_basis, partial, gram)
    payload = summed(payload, "gz")
    payload = summed(payload, "gx")
    parts = summed(payload, "gy", last=True)
    projected, coefficients = call(
        "project",
        project,
        (like((16, 16, 8, 128)), like((16, 32))),
        scratch=[pltpu.VMEM((16, 16, 8, 128), F32), pltpu.SemaphoreType.DMA((8,))],
        flops=1 << 28,
        data=3 << 20,
        specs={
            "out_specs": (
                pl.BlockSpec(memory_space=pl.ANY),
                pl.BlockSpec(memory_space=pltpu.VMEM),
            )
        },
    )(parts, image, columns, flat)
    return projected, coefficients.T


def solution(mesh):
    in_specs = (
        P(None, "gx", "gy", "gz"),
        P(None, "gx", "gy", "gz"),
        P("gx", "gy", "gz"),
        P(None, "gx", "gy", "gz"),
    )
    out_specs = (P(None, "gx", "gy", "gz"), P())
    return jax.shard_map(local, mesh=mesh, in_specs=in_specs, out_specs=out_specs, check_vma=False)
```
